32 devices in a mesh: seq: 16 (over z, x, core), head: 2 (over y).
Axes of the slice: x: 2, y: 2, z: 4, core: 2. Of those that a mesh axis runs over, the one named last changes fastest.
Arguments:
- channels_in: bfloat16 [2, 12288, 2560], P(None, 'seq', 'head'), may hold values from -6 to 6
- gate_in: bfloat16 [2, 12288, 2560], P(None, 'seq', 'head'), may hold values from -30 to 30
- projections: bfloat16 [2, 2, 12288, 128], P(None, None, 'seq'), may hold values from -1.796875 to 1.796875
- step_raw: bfloat16 [2, 40, 12288], P(None, 'head', 'seq'), may hold values from -4 to 4
- decay_log: float32 [40], P('head'), may hold values from -7 to 2
- step_bias: float32 [40], P('head'), may hold values from -7 to -1
- skip_gain: float32 [40], P('head'), may hold values from 0.3 to 1.2
- norm_gain: float32 [2560], P('head'), may hold values from 0.25 to 1.75
- out_weight: bfloat16 [2560, 1280], P('head'), may hold values from -0.15625 to 0.15625
Outputs:
- mixed: bfloat16 [12288, 2560], P('seq', 'head')
The draws below stay inside these ranges and needn't reach their ends.
All inputs are finite; a program needn't handle non-finite values.
Results may differ from the reference program's by a relative error of at most 0.017.
Values may be sent and summed in bfloat16 or wider, within the bound.
A program may use at most 128 MiB of HBM per device.

```python
import math
import jax
import jax.numpy as jnp
from jax import lax

HEADS = 40
P_SIZE = 64
N = 128
HALF = 1280
Q = 256
TOK_DEV = 768
TOKENS = 12288
INNER = 2560
N_HEAD = 2


def head_kinds(key):
    folded = jax.random.fold_in(key, 11)
    ranking = jax.random.permutation(folded, HEADS)
    fast_count = HEADS // 2
    return ranking < fast_count


def slow_step():
    return 0.1 * math.sqrt(40.0 / TOKENS)


def draw_step_bias(key, part):
    fast_mask = head_kinds(key)
    jitter = jax.random.uniform(jax.random.fold_in(key, 12), (HEADS,), jnp.float32, -0.3, 0.3)
    target_step = jnp.where(fast_mask, 0.1, slow_step())
    return (jnp.log(jnp.expm1(target_step)) + jitter).astype(jnp.float32)


def draw_decay_log(key, part):
    fast_mask = head_kinds(key)
    spread = jax.random.uniform(jax.random.fold_in(key, 13), (HEADS,), jnp.float32, 0.0, 1.0)
    fast_rate = 60.0 / Q * jnp.exp(math.log(0.6) + spread * math.log(1.6 / 0.6))
    slow_rate = 0.3 / TOKENS * jnp.exp(spread * math.log(4.0)) / slow_step()
    return jnp.log(jnp.where(fast_mask, fast_rate, slow_rate)).astype(jnp.float32)


def draw_step_raw(key, part):
    shape = (2, HEADS, TOKENS)
    rough_part = jnp.clip(0.6 * jax.random.normal(jax.random.fold_in(key, 14), shape, jnp.float32), -2.4, 2.4)
    block_offsets = jax.random.uniform(jax.random.fold_in(key, 15), (2, HEADS, TOKENS // TOK_DEV), jnp.float32, -0.7, 0.7)
    block_index = jnp.arange(TOKENS) // TOK_DEV
    return (rough_part + block_offsets[:, :, block_index]).astype(jnp.bfloat16)


def draw_gate_in(key, part):
    shape = (2, TOKENS, INNER)
    base_draw = jnp.clip(jax.random.normal(jax.random.fold_in(key, 16), shape, jnp.float32), -3.0, 3.0)
    column_place = jnp.arange(INNER).astype(jnp.float32) / INNER
    column_jitter = jax.random.uniform(jax.random.fold_in(key, 17), (2, 1, INNER), jnp.float32, 0.0, 1.0)
    column_scale = jnp.exp(math.log(10.0) * (0.5 * column_place[None, None, :] + 0.5 * column_jitter))
    row_scale = jnp.exp(math.log(10.0) * jax.random.uniform(jax.random.fold_in(key, 18), (2, TOKENS, 1), jnp.float32, 0.0, 1.0))
    return (base_draw * column_scale * row_scale / 10.0).astype(jnp.bfloat16)


def spiked(result, stream_key, source, target, shards_of, factor):
    owner, partner = [(jnp.arange(result.shape[position]) // (result.shape[position] // shards_of)).reshape([-1 if axis == position else 1 for axis in range(result.ndim)]) for position in (source, target)]
    chosen = jax.random.permutation(stream_key, shards_of)[partner]
    strong = (owner == chosen) | (owner == (partner + shards_of // 2) % shards_of)
    return jnp.where(strong, factor * result, result)


def level_of(own_key, extent, split, smallest, high):
    factor_of, own = 1.0, jax.random.fold_in(own_key, 6)
    for dim, parts in split:
        draws = jnp.exp(jax.random.uniform(jax.random.fold_in(own, dim), (parts,), jnp.float32, smallest / len(split), high / len(split)))
        factor_of = factor_of * jnp.repeat(draws, extent[dim] // parts).reshape([-1 if axis == dim else 1 for axis in range(len(extent))])
    return factor_of


def gaussian(own_key, shape, deviation, reach, split=(), held_as=jnp.bfloat16):
    result = deviation * jax.random.normal(own_key, shape, jnp.float32)
    if split:
        result = result * level_of(own_key, shape, split, -0.22, 0.18)
    return jnp.clip(result, -reach, reach).astype(held_as)


def gaussian_with(stream_key, dims, deviation, most, shards, heavy, held_as=jnp.bfloat16):
    array = deviation * jax.random.normal(stream_key, dims, jnp.float32)
    if shards:
        array = array * level_of(stream_key, dims, shards, -0.22, 0.18)
    return jnp.clip(spiked(array, jax.random.fold_in(stream_key, 3), *heavy), -most, most).astype(held_as)


def setup_inputs(seed: int = 0) -> dict:
    seeds = jax.random.split(jax.random.key(seed), 10)
    channels_in = gaussian(seeds[0], (2, TOKENS, INNER), 1.0, 6.0, ((1, 16), (2, 2)))
    gate_in = draw_gate_in(jax.random.fold_in(seeds[9], 71), 0)
    projections = gaussian(seeds[2], (2, 2, TOKENS, N), 0.3, 1.796875, ((2, 16),))
    step_raw = draw_step_raw(jax.random.fold_in(seeds[9], 71), 0)
    decay_log = draw_decay_log(jax.random.fold_in(seeds[9], 71), 0)
    step_bias = draw_step_bias(jax.random.fold_in(seeds[9], 71), 0)
    skip_gain = jnp.clip(0.3 + 0.90000004 * jax.random.uniform(seeds[6], (HEADS,), jnp.float32) ** level_of(seeds[6], (HEADS,), ((0, 2),), -0.2, 0.2), 0.3, 1.2)
    norm_gain = jnp.clip(1.0 + 0.15 * jax.random.normal(seeds[7], (INNER,), jnp.float32), 0.25, 1.75)
    out_weight = gaussian_with(seeds[8], (INNER, HALF), INNER ** -0.5, 0.15625, ((0, 2),), (0, 1, 2, 2.0))
    return dict(channels_in=channels_in, gate_in=gate_in, projections=projections, step_raw=step_raw, decay_log=decay_log, step_bias=step_bias, skip_gain=skip_gain, norm_gain=norm_gain, out_weight=out_weight)


def scan_direction(channels, write_rows, read_rows, step_raw, decay_log, step_bias, skip_gain):
    total_rows = channels.shape[0]
    block_count = total_rows // Q
    step_size = jax.nn.softplus(step_raw.astype(jnp.float32) + step_bias[:, None])
    log_decay = -step_size * jnp.exp(decay_log)[:, None]
    values = channels.reshape(block_count, Q, HEADS, P_SIZE)
    write_blocks = write_rows.reshape(block_count, Q, N)
    read_blocks = read_rows.reshape(block_count, Q, N)
    step_blocks = step_size.reshape(HEADS, block_count, Q).transpose(1, 0, 2)
    decay_blocks = log_decay.reshape(HEADS, block_count, Q).transpose(1, 0, 2)
    causal = jnp.arange(Q)[:, None] >= jnp.arange(Q)[None, :]

    def one_block(carried, pieces):
        value_block, write_block, read_block, step_block, decay_block = pieces
        cumulative = jnp.cumsum(decay_block, axis=1)
        scores = jnp.dot(read_block, write_block.T, preferred_element_type=jnp.float32)
        spread = jnp.where(causal[None], cumulative[:, :, None] - cumulative[:, None, :], 0.0)
        weights = jnp.where(causal[None], jnp.exp(spread), 0.0) * scores[None] * step_block[:, None, :]
        weights = weights.astype(jnp.bfloat16)
        within = jnp.einsum('hts,shp->thp', weights.astype(jnp.float32), value_block.astype(jnp.float32))
        entry_state = carried.astype(jnp.bfloat16)
        carried_part = jnp.einsum('tn,hnp->thp', read_block.astype(jnp.float32), entry_state.astype(jnp.float32))
        carried_part = carried_part * jnp.exp(cumulative).T[:, :, None]
        summed = within + carried_part + skip_gain[None, :, None] * value_block.astype(jnp.float32)
        tail_weight = jnp.exp(cumulative[:, -1:] - cumulative) * step_block
        loaded = (write_block.astype(jnp.float32)[None] * tail_weight[:, :, None]).astype(jnp.bfloat16)
        fresh_state = jnp.einsum('hsn,shp->hnp', loaded.astype(jnp.float32), value_block.astype(jnp.float32))
        carried = jnp.exp(cumulative[:, -1])[:, None, None] * carried + fresh_state
        return (carried, summed.astype(jnp.bfloat16).reshape(Q, HEADS * P_SIZE))
    initial = jnp.zeros((HEADS, N, P_SIZE), jnp.float32)
    final_state, outputs = lax.scan(one_block, initial, (values, write_blocks, read_blocks, step_blocks, decay_blocks))
    return outputs.reshape(total_rows, HEADS * P_SIZE)

def reference(channels_in, gate_in, projections, step_raw, decay_log, step_bias, skip_gain, norm_gain, out_weight):
    forward = scan_direction(channels_in[0], projections[0, 0], projections[0, 1], step_raw[0], decay_log, step_bias, skip_gain)
    backward = scan_direction(channels_in[1][::-1], projections[1, 0][::-1], projections[1, 1][::-1], step_raw[1][:, ::-1], decay_log, step_bias, skip_gain)[::-1]
    scanned = jnp.stack([forward, backward]).astype(jnp.float32)
    gated_rows = scanned * jax.nn.silu(gate_in.astype(jnp.float32))
    squares = lax.optimization_barrier(jnp.sum(gated_rows * gated_rows, axis=2, keepdims=True))
    normed = (gated_rows * lax.rsqrt(squares / INNER + 1e-05) * norm_gain).astype(jnp.bfloat16)
    group_width = INNER // N_HEAD
    weight_groups = out_weight.reshape(N_HEAD, group_width, HALF)
    normed_groups = normed.reshape(2, TOKENS, N_HEAD, group_width).transpose(2, 0, 1, 3)

    def add_group(summed, pieces):
        normed_piece, weight_piece = pieces
        forward_part = jnp.dot(normed_piece[0], weight_piece, preferred_element_type=jnp.float32)
        reverse_part = jnp.dot(normed_piece[1], weight_piece, preferred_element_type=jnp.float32)[:, ::-1]
        rounded = lax.optimization_barrier(jnp.concatenate([forward_part, reverse_part], axis=1).astype(jnp.bfloat16))
        return (summed + rounded.astype(jnp.float32), None)
    initial = jnp.zeros((TOKENS, 2 * HALF), jnp.float32)
    summed, unused = lax.scan(add_group, initial, (normed_groups, weight_groups))
    return summed.astype(jnp.bfloat16)
```

```python
import functools

import jax
import jax.numpy as jnp
from jax import lax
from jax.experimental import pallas as pl
from jax.experimental.pallas import tpu as pltpu
from jax.sharding import PartitionSpec as P

SUB = 128
PAD = 16
EPS = 1e-05
F32 = jnp.float32
BF16 = jnp.bfloat16


def padded(heads):
    return -(-heads // 8) * 8


def cumulate(values, backward):
    lane = lax.broadcasted_iota(jnp.int32, values.shape, 1)
    own = values
    reach = 1
    while reach < SUB:
        values = values + jnp.where(lane >= reach, pltpu.roll(values, reach, axis=1), 0.0)
        reach *= 2
    total = jnp.broadcast_to(values[:, SUB - 1 :], values.shape)
    if isinstance(backward, bool):
        return (total - values + own if backward else values), total
    return jnp.where(backward, total - values + own, values), total


def steps_of(raw, params):
    step = raw + params[:, 1:2]
    step = jnp.maximum(step, 0.0) + jnp.log1p(jnp.exp(-jnp.abs(step)))
    return step, -step * jnp.exp(params[:, 0:1])


def spreader(rows, columns, width):
    row = lax.broadcasted_iota(jnp.int32, (rows, columns), 0) * width
    column = lax.broadcasted_iota(jnp.int32, (rows, columns), 1)
    one = jnp.where((column >= row) & (column < row + width), 1.0, 0.0)
    return jnp.concatenate([one, one], axis=0).astype(BF16)


def spread(by_head, spread_matrix):
    high = by_head.astype(BF16).astype(F32)
    both = jnp.concatenate([high, by_head - high], axis=0).T.astype(BF16)
    return jnp.dot(both, spread_matrix, preferred_element_type=F32)


def totals_kernel(width, x_ref, b_ref, raw_ref, params_ref, out_ref, raw_scr, scaled):
    heads = raw_ref.shape[1]
    tokens, channels = x_ref.shape[1:]
    state = b_ref.shape[-1]
    raw_scr[...] = jnp.zeros_like(raw_scr)
    raw_scr[:heads, :] = raw_ref[0].astype(F32)
    params = params_ref[...]
    matrix = spreader(raw_scr.shape[0], channels, width)
    backward = pl.program_id(0) == 1
    count = tokens // SUB
    pieces = []
    everything = jnp.zeros((raw_scr.shape[0], SUB), F32)
    for k in range(count):
        step, log_decay = steps_of(raw_scr[:, k * SUB : (k + 1) * SUB], params)
        cumulative, total = cumulate(log_decay, backward)
        pieces.append((step, cumulative, total))
        everything = everything + total
    zero = jnp.zeros_like(everything)
    earlier, later = [zero], [zero]
    for k in range(count - 1):
        earlier.append(earlier[-1] + pieces[k][2])
        later.append(later[-1] + pieces[count - 1 - k][2])
    for k in range(count):
        step, cumulative, total = pieces[k]
        rest = jnp.where(backward, earlier[k], later[count - 1 - k])
        tail = jnp.exp(rest + total - cumulative) * step
        rows = slice(k * SUB, (k + 1) * SUB)
        scaled[rows, :] = (x_ref[0, rows, :].astype(F32) * spread(tail, matrix)).astype(BF16)
    summed = lax.dot_general(
        b_ref[0, 0], scaled[...], (((0,), (0,)), ((), ())), preferred_element_type=F32
    )
    out_ref[0, :state, :] = summed.astype(BF16)
    logs = spread(everything, matrix)[:PAD, :]
    high = logs.astype(BF16).astype(F32)
    row = lax.broadcasted_iota(jnp.int32, logs.shape, 0)
    out_ref[0, state:, :] = jnp.where(row == 0, high, logs - high).astype(BF16)


def carry_kernel(fwd_ref, bwd_ref, out_ref):
    j = pl.program_id(0)
    count = pl.num_programs(0)
    me = lax.axis_index("seq")
    state = out_ref.shape[1]

    @pl.when(j == 0)
    def _():
        out_ref[...] = jnp.zeros_like(out_ref)

    def link(d, ref):
        logs = ref[0, 0, state : state + PAD, :].astype(F32)
        decay = jnp.exp(logs[0:1, :] + logs[1:2, :])
        out_ref[d] = out_ref[d] * decay + ref[0, 0, :state, :].astype(F32)

    @pl.when(j < me)
    def _():
        link(0, fwd_ref)

    @pl.when(count - 1 - j > me)
    def _():
        link(1, bwd_ref)


def scan_kernel(
    width, d_ref, x_ref, gate_ref, b_ref, c_ref, raw_ref, params_ref, gain_ref, w_ref, carry_ref,
    part_ref, square_ref, raw_scr, state_scr, summed,
):
    heads = raw_ref.shape[1]
    rows, channels = x_ref.shape[1:]
    d = d_ref[0]
    backward = d == 1
    params = params_ref[...]
    head_rows = raw_scr.shape[0]
    matrix = spreader(head_rows, channels, width)

    @pl.when(pl.program_id(0) == 0)
    def _():
        state_scr[...] = carry_ref[0]

    raw_scr[...] = jnp.zeros_like(raw_scr)
    raw_scr[:heads, :] = raw_ref[0].astype(F32)
    skip = spread(jnp.broadcast_to(params[:, 2:3], (head_rows, SUB)), matrix)[0:1, :]
    t_index = lax.broadcasted_iota(jnp.int32, (SUB, SUB), 0)
    s_index = lax.broadcasted_iota(jnp.int32, (SUB, SUB), 1)
    sign = 1 - 2 * d
    seen = (t_index - s_index) * sign >= 0
    lane = lax.broadcasted_iota(jnp.int32, (SUB, 2 * width), 1)
    low = jnp.where(lane < width, 1.0, 0.0).astype(BF16)
    high = jnp.where(lane >= width, 1.0, 0.0).astype(BF16)
    subs = rows // SUB
    for i in range(subs):
        at = pl.multiple_of((i + d * (subs - 1 - 2 * i)) * SUB, SUB)
        here = pl.ds(at, SUB)
        step, log_decay = steps_of(raw_scr[:, here], params)
        cumulative, total = cumulate(log_decay, backward)
        rowterm = cumulative - jnp.log(step)
        columns = cumulative.T
        entry_decay = spread(jnp.exp(cumulative), matrix)
        tail = spread(jnp.exp(total - cumulative) * step, matrix)
        read = c_ref[0, 0, here, :]
        write = b_ref[0, 0, here, :]
        scores = lax.dot_general(
            read, write, (((1,), (1,)), ((), ())), preferred_element_type=F32
        )
        x = x_ref[0, here, :]
        wide = x.astype(F32)
        carried = jnp.dot(read, state_scr[...].astype(BF16), preferred_element_type=F32)
        summed[here, :] = carried * entry_decay + skip * wide
        for first in range(0, heads, 2):
            weights = []
            for h in range(first, min(first + 2, heads)):
                power = jnp.where(seen, columns[:, h : h + 1] - rowterm[h : h + 1, :], -1e30)
                weights.append((jnp.exp(power) * scores).astype(BF16))
            span = slice(first * width, (first + len(weights)) * width)
            some_x = x[:, span]
            if len(weights) == 2:
                weights = [jnp.concatenate(weights, axis=1)]
                some_x = jnp.concatenate([some_x * low, some_x * high], axis=0)
            summed[here, span] += jnp.dot(weights[0], some_x, preferred_element_type=F32)
        fresh = lax.dot_general(
            write, (wide * tail).astype(BF16), (((0,), (0,)), ((), ())),
            preferred_element_type=F32,
        )
        decay = jnp.where(backward, entry_decay[0:1, :], entry_decay[SUB - 1 :, :])
        state_scr[...] = state_scr[...] * decay + fresh
    scanned = summed[...].astype(BF16).astype(F32)
    gate = gate_ref[0].astype(F32)
    gated = scanned * (gate / (1.0 + jnp.exp(-gate)))
    square_ref[...] = jnp.sum(gated * gated, axis=1, keepdims=True)
    part = jnp.dot(
        (gated * gain_ref[...]).astype(BF16), w_ref[...], preferred_element_type=F32
    ).astype(BF16)

    @pl.when(d == 0)
    def _():
        part_ref[...] = part

    @pl.when(d == 1)
    def _():
        flip = jnp.where(t_index + s_index == SUB - 1, 1.0, 0.0).astype(BF16)
        blocks = part.shape[1] // SUB
        for k in range(blocks):
            taken = part[:, (blocks - 1 - k) * SUB : (blocks - k) * SUB]
            part_ref[:, k * SUB : (k + 1) * SUB] = jnp.dot(
                taken, flip, preferred_element_type=F32
            ).astype(BF16)


def per_device(
    channels_in, gate_in, projections, step_raw, decay_log, step_bias, skip_gain, norm_gain,
    out_weight,
):
    tokens, channels = channels_in.shape[1:]
    heads = step_raw.shape[1]
    width = channels // heads
    state = projections.shape[-1]
    half = out_weight.shape[1]
    groups = lax.axis_size("head")
    inner = groups * channels
    devices = lax.axis_size("seq")
    block = 2 * SUB if tokens % (2 * SUB) == 0 else SUB
    blocks = tokens // block
    head_rows = padded(heads)
    params = jnp.pad(
        jnp.stack([decay_log, step_bias, skip_gain], axis=1), ((0, head_rows - heads), (0, 0))
    )

    totals = pl.pallas_call(
        functools.partial(totals_kernel, width),
        out_shape=jax.ShapeDtypeStruct((2, state + PAD, channels), BF16),
        grid=(2,),
        in_specs=[
            pl.BlockSpec((1, tokens, channels), lambda d: (d, 0, 0)),
            pl.BlockSpec((1, 1, tokens, state), lambda d: (d, 0, 0, 0)),
            pl.BlockSpec((1, heads, tokens), lambda d: (d, 0, 0)),
            pl.BlockSpec((head_rows, 3), lambda d: (0, 0)),
        ],
        out_specs=pl.BlockSpec((1, state + PAD, channels), lambda d: (d, 0, 0)),
        scratch_shapes=[pltpu.VMEM((head_rows, tokens), F32), pltpu.VMEM((tokens, channels), BF16)],
        name="totals",
    )(channels_in, projections, step_raw, params)

    gathered = lax.all_gather(totals, "seq")
    carries = pl.pallas_call(
        carry_kernel,
        out_shape=jax.ShapeDtypeStruct((2, state, channels), F32),
        grid=(devices,),
        in_specs=[
            pl.BlockSpec((1, 1, state + PAD, channels), lambda j: (j, 0, 0, 0)),
            pl.BlockSpec((1, 1, state + PAD, channels), lambda j: (devices - 1 - j, 1, 0, 0)),
        ],
        out_specs=pl.BlockSpec((2, state, channels), lambda j: (0, 0, 0)),
        name="carry",
    )(gathered, gathered)

    def place(k, d):
        return k + d[0] * (blocks - 1 - 2 * k)

    def scan(d):
        return pl.pallas_call(
            functools.partial(scan_kernel, width),
            out_shape=(
                jax.ShapeDtypeStruct((tokens, half), BF16),
                jax.ShapeDtypeStruct((tokens, 1), F32),
            ),
            grid_spec=pltpu.PrefetchScalarGridSpec(
                num_scalar_prefetch=1,
                grid=(blocks,),
                in_specs=[
                    pl.BlockSpec((1, block, channels), lambda k, d: (d[0], place(k, d), 0)),
                    pl.BlockSpec((1, block, channels), lambda k, d: (d[0], place(k, d), 0)),
                    pl.BlockSpec((1, 1, block, state), lambda k, d: (d[0], 0, place(k, d), 0)),
                    pl.BlockSpec((1, 1, block, state), lambda k, d: (d[0], 1, place(k, d), 0)),
                    pl.BlockSpec((1, heads, block), lambda k, d: (d[0], 0, place(k, d))),
                    pl.BlockSpec((head_rows, 3), lambda k, d: (0, 0)),
                    pl.BlockSpec((1, channels), lambda k, d: (0, 0)),
                    pl.BlockSpec((channels, half), lambda k, d: (0, 0)),
                    pl.BlockSpec((1, state, channels), lambda k, d: (d[0], 0, 0)),
                ],
                out_specs=[
                    pl.BlockSpec((block, half), lambda k, d: (place(k, d), 0)),
                    pl.BlockSpec((block, 1), lambda k, d: (place(k, d), 0)),
                ],
                scratch_shapes=[
                    pltpu.VMEM((head_rows, block), F32),
                    pltpu.VMEM((state, channels), F32),
                    pltpu.VMEM((block, channels), F32),
                ],
            ),
            cost_estimate=pl.CostEstimate(
                flops=4 * tokens * channels * half,
                bytes_accessed=6 * tokens * channels + 2 * channels * half,
                transcendentals=0,
            ),
            name="scan",
        )(
            d.astype(jnp.int32).reshape(1), channels_in, gate_in, projections, projections,
            step_raw, params, norm_gain[None], out_weight, carries,
        )

    group = lax.axis_index("head")
    if groups == 2:
        swap = [(0, 1), (1, 0)]
        part, square = scan(1 - group)
        part = lax.ppermute(part, "head", swap)
        square = lax.ppermute(square, "head", swap)
        own_part, own_square = scan(group)
        summed = own_part.astype(F32) + part.astype(F32)
        squares = own_square + square
    else:
        results = [scan(jnp.asarray(d)) for d in range(2)]
        summed = lax.psum_scatter(
            jnp.concatenate([results[0][0], results[1][0]], axis=1),
            "head", scatter_dimension=1, tiled=True,
        ).astype(F32)
        both = lax.psum(jnp.stack([results[0][1], results[1][1]]), "head")
        squares = jnp.where(2 * group >= groups, both[1], both[0])
    return (summed * lax.rsqrt(squares / inner + EPS)).astype(BF16)


def solution(mesh):
    placed = (
        P(None, "seq", "head"),
        P(None, "seq", "head"),
        P(None, None, "seq", None),
        P(None, "head", "seq"),
        P("head"),
        P("head"),
        P("head"),
        P("head"),
        P("head", None),
    )
    return jax.shard_map(
        per_device, mesh=mesh, in_specs=placed, out_specs=P("seq", "head"), check_vma=False
    )
```

```python
import functools
import math

import jax
import jax.numpy as jnp
from jax import lax
from jax.experimental import pallas as pl
from jax.experimental.pallas import tpu as pltpu
from jax.sharding import PartitionSpec as P

SUB = 128
PAD = 16
EPS = 1e-05
F32 = jnp.float32
BF16 = jnp.bfloat16


def padded(heads):
    return -(-heads // 8) * 8


def cumulate(values, backward):
    lane = lax.broadcasted_iota(jnp.int32, values.shape, 1)
    own = values
    reach = 1
    while reach < SUB:
        values = values + jnp.where(lane >= reach, pltpu.roll(values, reach, axis=1), 0.0)
        reach *= 2
    total = jnp.broadcast_to(values[:, SUB - 1 :], values.shape)
    if isinstance(backward, bool):
        return (total - values + own if backward else values), total
    return jnp.where(backward, total - values + own, values), total


def steps_of(raw, params):
    step = raw + params[:, 1:2]
    step = jnp.maximum(step, 0.0) + jnp.log1p(jnp.exp(-jnp.abs(step)))
    return step, -step * jnp.exp(params[:, 0:1])


def spreader(rows, columns, width):
    row = lax.broadcasted_iota(jnp.int32, (rows, columns), 0) * width
    column = lax.broadcasted_iota(jnp.int32, (rows, columns), 1)
    one = jnp.where((column >= row) & (column < row + width), 1.0, 0.0)
    return jnp.concatenate([one, one], axis=0).astype(BF16)


def spread(by_head, spread_matrix):
    high = by_head.astype(BF16).astype(F32)
    both = jnp.concatenate([high, by_head - high], axis=0).T.astype(BF16)
    return jnp.dot(both, spread_matrix, preferred_element_type=F32)


def totals_kernel(
    width, x_ref, b_ref, raw_ref, params_ref, out_ref, log_ref, raw_scr, scaled
):
    heads = raw_ref.shape[1]
    tokens, channels = x_ref.shape[1:]
    state = b_ref.shape[-1]
    raw_scr[...] = jnp.zeros_like(raw_scr)
    raw_scr[:heads, :] = raw_ref[0].astype(F32)
    params = params_ref[...]
    matrix = spreader(raw_scr.shape[0], channels, width)
    backward = pl.program_id(0) == 1
    count = tokens // SUB
    pieces = []
    everything = jnp.zeros((raw_scr.shape[0], SUB), F32)
    for k in range(count):
        step, log_decay = steps_of(raw_scr[:, k * SUB : (k + 1) * SUB], params)
        cumulative, total = cumulate(log_decay, backward)
        pieces.append((step, cumulative, total))
        everything = everything + total
    zero = jnp.zeros_like(everything)
    earlier, later = [zero], [zero]
    for k in range(count - 1):
        earlier.append(earlier[-1] + pieces[k][2])
        later.append(later[-1] + pieces[count - 1 - k][2])
    for k in range(count):
        step, cumulative, total = pieces[k]
        rest = jnp.where(backward, earlier[k], later[count - 1 - k])
        tail = jnp.exp(rest + total - cumulative) * step
        rows = slice(k * SUB, (k + 1) * SUB)
        scaled[rows, :] = (x_ref[0, rows, :].astype(F32) * spread(tail, matrix)).astype(BF16)
    summed = lax.dot_general(
        b_ref[0, 0], scaled[...], (((0,), (0,)), ((), ())), preferred_element_type=F32
    )
    out_ref[0] = summed.astype(BF16)
    rest = jnp.zeros((SUB - everything.shape[0], SUB), F32)
    log_ref[0] = packed_row(jnp.concatenate([everything, rest], axis=0).T[0:1, :])


def packed_row(row):
    row = jnp.broadcast_to(row, (PAD, row.shape[1]))
    high = row.astype(BF16).astype(F32)
    index = lax.broadcasted_iota(jnp.int32, row.shape, 0)
    return jnp.where(index == 0, high, jnp.where(index == 1, row - high, 0.0)).astype(BF16)


def carry_kernel(
    width, mates, planes, state_ref, log_ref, out_ref, one_state, one_log, sum_state, sum_log,
    two_state, two_log, entry, mine, three_state, send_sem, recv_sem,
):
    device = lax.axis_index("seq")
    plane, spot = device // mates, device % mates
    rows = one_state.shape[2]
    channels = state_ref.shape[-1]
    matrix = spreader(SUB, channels, width)[:SUB]

    def remote(source, target, which, slot, device_id):
        return pltpu.make_async_remote_copy(
            src_ref=source, dst_ref=target, send_sem=send_sem.at[which],
            recv_sem=recv_sem.at[slot], device_id={"seq": device_id},
            device_id_type=pl.DeviceIdType.MESH,
        )

    def rows_of(q):
        return pl.ds(pl.multiple_of(q * rows, rows), rows)

    def decay_of(packed):
        both = jnp.dot(packed, matrix, preferred_element_type=F32)
        return jnp.exp(both[0:1, :] + both[1:2, :])

    others = [(spot + o) % mates for o in range(1, mates)]
    far = [(plane + o) % planes for o in range(1, planes)]
    barrier = pltpu.get_barrier_semaphore()
    for q in others:
        pl.semaphore_signal(
            barrier, inc=1, device_id={"seq": plane * mates + q},
            device_id_type=pl.DeviceIdType.MESH,
        )
    for p in far:
        pl.semaphore_signal(
            barrier, inc=1, device_id={"seq": p * mates + spot},
            device_id_type=pl.DeviceIdType.MESH,
        )
    pl.semaphore_wait(barrier, mates + planes - 2)

    base = 0
    started = []
    for o, q in enumerate(others):
        to = plane * mates + q
        started.append(
            remote(state_ref.at[:, rows_of(q)], one_state.at[spot], base + 2 * o, base + 2 * spot, to)
        )
        started.append(
            remote(log_ref, one_log.at[spot], base + 2 * o + 1, base + 2 * spot + 1, to)
        )
    for copy in started:
        copy.start()
    one_state[spot] = state_ref[:, rows_of(spot), :]
    one_log[spot] = log_ref[...]
    for o, q in enumerate(others):
        remote(one_state.at[q], one_state.at[q], base + 2 * o, base + 2 * q, device).wait_recv()
        remote(one_log.at[q], one_log.at[q], base + 2 * o + 1, base + 2 * q + 1, device).wait_recv()

    decays = [[decay_of(one_log[q, d]) for q in range(mates)] for d in range(2)]
    orders = [list(range(mates)), list(range(mates))[::-1]]
    for d in range(2):
        total = None
        logs = None
        for q in orders[d]:
            part = one_state[q, d].astype(F32)
            log = one_log[q, d].astype(F32)
            total = part if total is None else total * decays[d][q] + part
            logs = log if logs is None else logs + log
        sum_state[d] = total.astype(BF16)
        sum_log[d] = packed_row(logs[0:1, :] + logs[1:2, :])
    base = 2 * mates
    for o, p in enumerate(far):
        d = jnp.where(p > plane, 0, 1)
        to = p * mates + spot
        for j, (source, target) in enumerate(((sum_state, two_state), (sum_log, two_log))):
            copy = remote(
                source.at[d], target.at[plane], base + 2 * o + j, base + 2 * plane + j, to
            )
            copy.start()
            started.append(copy)
    for o, p in enumerate(far):
        for j, target in enumerate((two_state, two_log)):
            remote(
                target.at[p], target.at[p], base + 2 * o + j, base + 2 * p + j, device
            ).wait_recv()
    entry[...] = jnp.zeros_like(entry)

    def link(d, p):
        entry[d] = entry[d] * decay_of(two_log[p]) + two_state[p].astype(F32)

    for p in range(planes):
        pl.when(p < plane)(functools.partial(link, 0, p))
        pl.when(planes - 1 - p > plane)(functools.partial(link, 1, planes - 1 - p))

    base = 2 * mates + 2 * planes
    for d in range(2):
        carried = entry[d]
        for q in orders[d]:
            mine[q, d] = carried.astype(BF16)
            if q != orders[d][-1]:
                carried = carried * decays[d][q] + one_state[q, d].astype(F32)
    for o, q in enumerate(others):
        copy = remote(mine.at[q], three_state.at[spot], base + o, base + spot, plane * mates + q)
        copy.start()
        started.append(copy)
    three_state[spot] = mine[spot]
    for o, q in enumerate(others):
        remote(three_state.at[q], three_state.at[q], base + o, base + q, device).wait_recv()
    for q in range(mates):
        for d in range(2):
            out_ref[d, q * rows : (q + 1) * rows, :] = three_state[q, d].astype(F32)
    for copy in started:
        copy.wait_send()


def scan_kernel(
    width, d_ref, x_ref, gate_ref, b_ref, c_ref, raw_ref, params_ref, gain_ref, w_ref, carry_ref,
    part_ref, square_ref, raw_scr, state_scr, summed,
):
    heads = raw_ref.shape[1]
    rows, channels = x_ref.shape[1:]
    d = d_ref[0]
    backward = d == 1
    params = params_ref[...]
    head_rows = raw_scr.shape[0]
    matrix = spreader(head_rows, channels, width)

    @pl.when(pl.program_id(0) == 0)
    def _():
        state_scr[...] = carry_ref[0]

    raw_scr[...] = jnp.zeros_like(raw_scr)
    raw_scr[:heads, :] = raw_ref[0].astype(F32)
    skip = spread(jnp.broadcast_to(params[:, 2:3], (head_rows, SUB)), matrix)[0:1, :]
    t_index = lax.broadcasted_iota(jnp.int32, (SUB, SUB), 0)
    s_index = lax.broadcasted_iota(jnp.int32, (SUB, SUB), 1)
    sign = 1 - 2 * d
    seen = (t_index - s_index) * sign >= 0
    lane = lax.broadcasted_iota(jnp.int32, (SUB, 2 * width), 1)
    low = jnp.where(lane < width, 1.0, 0.0).astype(BF16)
    high = jnp.where(lane >= width, 1.0, 0.0).astype(BF16)
    subs = rows // SUB
    for i in range(subs):
        at = pl.multiple_of((i + d * (subs - 1 - 2 * i)) * SUB, SUB)
        here = pl.ds(at, SUB)
        step, log_decay = steps_of(raw_scr[:, here], params)
        cumulative, total = cumulate(log_decay, backward)
        rowterm = cumulative - jnp.log(step)
        columns = cumulative.T
        entry_decay = spread(jnp.exp(cumulative), matrix)
        tail = spread(jnp.exp(total - cumulative) * step, matrix)
        read = c_ref[0, 0, here, :]
        write = b_ref[0, 0, here, :]
        scores = lax.dot_general(
            read, write, (((1,), (1,)), ((), ())), preferred_element_type=F32
        )
        x = x_ref[0, here, :]
        wide = x.astype(F32)
        carried = jnp.dot(read, state_scr[...].astype(BF16), preferred_element_type=F32)
        summed[here, :] = carried * entry_decay + skip * wide
        for first in range(0, heads, 2):
            weights = []
            for h in range(first, min(first + 2, heads)):
                power = jnp.where(seen, columns[:, h : h + 1] - rowterm[h : h + 1, :], -1e30)
                weights.append((jnp.exp(power) * scores).astype(BF16))
            span = slice(first * width, (first + len(weights)) * width)
            some_x = x[:, span]
            if len(weights) == 2:
                weights = [jnp.concatenate(weights, axis=1)]
                some_x = jnp.concatenate([some_x * low, some_x * high], axis=0)
            summed[here, span] += jnp.dot(weights[0], some_x, preferred_element_type=F32)
        fresh = lax.dot_general(
            write, (wide * tail).astype(BF16), (((0,), (0,)), ((), ())),
            preferred_element_type=F32,
        )
        decay = jnp.where(backward, entry_decay[0:1, :], entry_decay[SUB - 1 :, :])
        state_scr[...] = state_scr[...] * decay + fresh
    scanned = summed[...].astype(BF16).astype(F32)
    gate = gate_ref[0].astype(F32)
    gated = scanned * (gate / (1.0 + jnp.exp(-gate)))
    square_ref[...] = jnp.sum(gated * gated, axis=1, keepdims=True)
    part = jnp.dot(
        (gated * gain_ref[...]).astype(BF16), w_ref[...], preferred_element_type=F32
    ).astype(BF16)

    @pl.when(d == 0)
    def _():
        part_ref[...] = part

    @pl.when(d == 1)
    def _():
        flip = jnp.where(t_index + s_index == SUB - 1, 1.0, 0.0).astype(BF16)
        blocks = part.shape[1] // SUB
        for k in range(blocks):
            taken = part[:, (blocks - 1 - k) * SUB : (blocks - k) * SUB]
            part_ref[:, k * SUB : (k + 1) * SUB] = jnp.dot(
                taken, flip, preferred_element_type=F32
            ).astype(BF16)


def per_device(
    channels_in, gate_in, projections, step_raw, decay_log, step_bias, skip_gain, norm_gain,
    out_weight,
):
    tokens, channels = channels_in.shape[1:]
    heads = step_raw.shape[1]
    width = channels // heads
    state = projections.shape[-1]
    half = out_weight.shape[1]
    groups = lax.axis_size("head")
    inner = groups * channels
    devices = lax.axis_size("seq")
    block = 2 * SUB if tokens % (2 * SUB) == 0 else SUB
    blocks = tokens // block
    head_rows = padded(heads)
    params = jnp.pad(
        jnp.stack([decay_log, step_bias, skip_gain], axis=1), ((0, head_rows - heads), (0, 0))
    )

    totals, logs = pl.pallas_call(
        functools.partial(totals_kernel, width),
        out_shape=(
            jax.ShapeDtypeStruct((2, state, channels), BF16),
            jax.ShapeDtypeStruct((2, PAD, SUB), BF16),
        ),
        grid=(2,),
        in_specs=[
            pl.BlockSpec((1, tokens, channels), lambda d: (d, 0, 0)),
            pl.BlockSpec((1, 1, tokens, state), lambda d: (d, 0, 0, 0)),
            pl.BlockSpec((1, heads, tokens), lambda d: (d, 0, 0)),
            pl.BlockSpec((head_rows, 3), lambda d: (0, 0)),
        ],
        out_specs=[
            pl.BlockSpec((1, state, channels), lambda d: (d, 0, 0)),
            pl.BlockSpec((1, PAD, SUB), lambda d: (d, 0, 0)),
        ],
        scratch_shapes=[pltpu.VMEM((head_rows, tokens), F32), pltpu.VMEM((tokens, channels), BF16)],
        name="totals",
    )(channels_in, projections, step_raw, params)

    mates = math.gcd(devices, 4)
    planes = devices // mates
    share = state // mates
    copies = 3 * mates + 2 * planes
    carries = pl.pallas_call(
        functools.partial(carry_kernel, width, mates, planes),
        out_shape=jax.ShapeDtypeStruct((2, state, channels), F32),
        in_specs=[pl.BlockSpec(memory_space=pltpu.VMEM)] * 2,
        out_specs=pl.BlockSpec(memory_space=pltpu.VMEM),
        scratch_shapes=[
            pltpu.VMEM((mates, 2, share, channels), BF16),
            pltpu.VMEM((mates, 2, PAD, SUB), BF16),
            pltpu.VMEM((2, share, channels), BF16),
            pltpu.VMEM((2, PAD, SUB), BF16),
            pltpu.VMEM((planes, share, channels), BF16),
            pltpu.VMEM((planes, PAD, SUB), BF16),
            pltpu.VMEM((2, share, channels), F32),
            pltpu.VMEM((mates, 2, share, channels), BF16),
            pltpu.VMEM((mates, 2, share, channels), BF16),
            pltpu.SemaphoreType.DMA((copies,)),
            pltpu.SemaphoreType.DMA((copies,)),
        ],
        compiler_params=pltpu.CompilerParams(collective_id=0, has_side_effects=True),
        name="carry",
    )(totals, logs)

    def place(k, d):
        return k + d[0] * (blocks - 1 - 2 * k)

    def scan(d):
        return pl.pallas_call(
            functools.partial(scan_kernel, width),
            out_shape=(
                jax.ShapeDtypeStruct((tokens, half), BF16),
                jax.ShapeDtypeStruct((tokens, 1), F32),
            ),
            grid_spec=pltpu.PrefetchScalarGridSpec(
                num_scalar_prefetch=1,
                grid=(blocks,),
                in_specs=[
                    pl.BlockSpec((1, block, channels), lambda k, d: (d[0], place(k, d), 0)),
                    pl.BlockSpec((1, block, channels), lambda k, d: (d[0], place(k, d), 0)),
                    pl.BlockSpec((1, 1, block, state), lambda k, d: (d[0], 0, place(k, d), 0)),
                    pl.BlockSpec((1, 1, block, state), lambda k, d: (d[0], 1, place(k, d), 0)),
                    pl.BlockSpec((1, heads, block), lambda k, d: (d[0], 0, place(k, d))),
                    pl.BlockSpec((head_rows, 3), lambda k, d: (0, 0)),
                    pl.BlockSpec((1, channels), lambda k, d: (0, 0)),
                    pl.BlockSpec((channels, half), lambda k, d: (0, 0)),
                    pl.BlockSpec((1, state, channels), lambda k, d: (d[0], 0, 0)),
                ],
                out_specs=[
                    pl.BlockSpec((block, half), lambda k, d: (place(k, d), 0)),
                    pl.BlockSpec((block, 1), lambda k, d: (place(k, d), 0)),
                ],
                scratch_shapes=[
                    pltpu.VMEM((head_rows, block), F32),
                    pltpu.VMEM((state, channels), F32),
                    pltpu.VMEM((block, channels), F32),
                ],
            ),
            cost_estimate=pl.CostEstimate(
                flops=4 * tokens * channels * half,
                bytes_accessed=6 * tokens * channels + 2 * channels * half,
                transcendentals=0,
            ),
            name="scan",
        )(
            d.astype(jnp.int32).reshape(1), channels_in, gate_in, projections, projections,
            step_raw, params, norm_gain[None], out_weight, carries,
        )

    group = lax.axis_index("head")
    if groups == 2:
        swap = [(0, 1), (1, 0)]
        part, square = scan(1 - group)
        part = lax.ppermute(part, "head", swap)
        square = lax.ppermute(square, "head", swap)
        own_part, own_square = scan(group)
        summed = own_part.astype(F32) + part.astype(F32)
        squares = own_square + square
    else:
        results = [scan(jnp.asarray(d)) for d in range(2)]
        summed = lax.psum_scatter(
            jnp.concatenate([results[0][0], results[1][0]], axis=1),
            "head", scatter_dimension=1, tiled=True,
        ).astype(F32)
        both = lax.psum(jnp.stack([results[0][1], results[1][1]]), "head")
        squares = jnp.where(2 * group >= groups, both[1], both[0])
    return (summed * lax.rsqrt(squares / inner + EPS)).astype(BF16)


def solution(mesh):
    placed = (
        P(None, "seq", "head"),
        P(None, "seq", "head"),
        P(None, None, "seq", None),
        P(None, "head", "seq"),
        P("head"),
        P("head"),
        P("head"),
        P("head"),
        P("head", None),
    )
    return jax.shard_map(
        per_device, mesh=mesh, in_specs=placed, out_specs=P("seq", "head"), check_vma=False
    )
```

```python
import functools
import math

import jax
import jax.numpy as jnp
from jax import lax
from jax.experimental import pallas as pl
from jax.experimental.pallas import tpu as pltpu
from jax.sharding import PartitionSpec as P

SUB = 128
PAD = 16
EPS = 1e-05
F32 = jnp.float32
BF16 = jnp.bfloat16


def padded(heads):
    return -(-heads // 8) * 8


def cumulate(values, backward):
    lane = lax.broadcasted_iota(jnp.int32, values.shape, 1)
    own = values
    reach = 1
    while reach < SUB:
        values = values + jnp.where(lane >= reach, pltpu.roll(values, reach, axis=1), 0.0)
        reach *= 2
    total = jnp.broadcast_to(values[:, SUB - 1 :], values.shape)
    if isinstance(backward, bool):
        return (total - values + own if backward else values), total
    return jnp.where(backward, total - values + own, values), total


def steps_of(raw, params):
    step = raw + params[:, 1:2]
    step = jnp.maximum(step, 0.0) + jnp.log1p(jnp.exp(-jnp.abs(step)))
    return step, -step * jnp.exp(params[:, 0:1])


def spreader(rows, columns, width):
    row = lax.broadcasted_iota(jnp.int32, (rows, columns), 0) * width
    column = lax.broadcasted_iota(jnp.int32, (rows, columns), 1)
    one = jnp.where((column >= row) & (column < row + width), 1.0, 0.0)
    return jnp.concatenate([one, one], axis=0).astype(BF16)


def spread(by_head, spread_matrix):
    high = by_head.astype(BF16).astype(F32)
    both = jnp.concatenate([high, by_head - high], axis=0).T.astype(BF16)
    return jnp.dot(both, spread_matrix, preferred_element_type=F32)


def totals_kernel(
    width, x_ref, b_ref, raw_ref, params_ref, out_ref, log_ref, raw_scr, scaled
):
    heads = raw_ref.shape[1]
    tokens, channels = x_ref.shape[1:]
    state = b_ref.shape[-1]
    raw_scr[...] = jnp.zeros_like(raw_scr)
    raw_scr[:heads, :] = raw_ref[0].astype(F32)
    params = params_ref[...]
    matrix = spreader(raw_scr.shape[0], channels, width)
    backward = pl.program_id(0) == 1
    count = tokens // SUB
    pieces = []
    everything = jnp.zeros((raw_scr.shape[0], SUB), F32)
    for k in range(count):
        step, log_decay = steps_of(raw_scr[:, k * SUB : (k + 1) * SUB], params)
        cumulative, total = cumulate(log_decay, backward)
        pieces.append((step, cumulative, total))
        everything = everything + total
    zero = jnp.zeros_like(everything)
    earlier, later = [zero], [zero]
    for k in range(count - 1):
        earlier.append(earlier[-1] + pieces[k][2])
        later.append(later[-1] + pieces[count - 1 - k][2])
    for k in range(count):
        step, cumulative, total = pieces[k]
        rest = jnp.where(backward, earlier[k], later[count - 1 - k])
        tail = jnp.exp(rest + total - cumulative) * step
        rows = slice(k * SUB, (k + 1) * SUB)
        scaled[rows, :] = (x_ref[0, rows, :].astype(F32) * spread(tail, matrix)).astype(BF16)
    summed = lax.dot_general(
        b_ref[0, 0], scaled[...], (((0,), (0,)), ((), ())), preferred_element_type=F32
    )
    out_ref[0] = summed.astype(BF16)
    rest = jnp.zeros((SUB - everything.shape[0], SUB), F32)
    log_ref[0] = packed_row(jnp.concatenate([everything, rest], axis=0).T[0:1, :])


def packed_row(row):
    row = jnp.broadcast_to(row, (PAD, row.shape[1]))
    high = row.astype(BF16).astype(F32)
    index = lax.broadcasted_iota(jnp.int32, row.shape, 0)
    return jnp.where(index == 0, high, jnp.where(index == 1, row - high, 0.0)).astype(BF16)


def carry_kernel(
    width, mates, planes, state_ref, log_ref, out_ref, one_state, one_log, sum_state, sum_log,
    two_state, two_log, entry, mine, three_state, send_sem, recv_sem,
):
    device = lax.axis_index("seq")
    plane, spot = device // mates, device % mates
    rows = one_state.shape[2]
    channels = state_ref.shape[-1]
    matrix = spreader(SUB, channels, width)[:SUB]

    def remote(source, target, which, slot, device_id):
        return pltpu.make_async_remote_copy(
            src_ref=source, dst_ref=target, send_sem=send_sem.at[which],
            recv_sem=recv_sem.at[slot], device_id={"seq": device_id},
            device_id_type=pl.DeviceIdType.MESH,
        )

    def rows_of(q):
        return pl.ds(pl.multiple_of(q * rows, rows), rows)

    def decay_of(packed):
        both = jnp.dot(packed, matrix, preferred_element_type=F32)
        return jnp.exp(both[0:1, :] + both[1:2, :])

    others = [(spot + o) % mates for o in range(1, mates)]
    far = [(plane + o) % planes for o in range(1, planes)]
    barrier = pltpu.get_barrier_semaphore()
    for q in others:
        pl.semaphore_signal(
            barrier, inc=1, device_id={"seq": plane * mates + q},
            device_id_type=pl.DeviceIdType.MESH,
        )
    for p in far:
        pl.semaphore_signal(
            barrier, inc=1, device_id={"seq": p * mates + spot},
            device_id_type=pl.DeviceIdType.MESH,
        )
    pl.semaphore_wait(barrier, mates + planes - 2)

    base = 0
    started = []
    for o, q in enumerate(others):
        to = plane * mates + q
        started.append(
            remote(state_ref.at[:, rows_of(q)], one_state.at[spot], base + 2 * o, base + 2 * spot, to)
        )
        started.append(
            remote(log_ref, one_log.at[spot], base + 2 * o + 1, base + 2 * spot + 1, to)
        )
    for copy in started:
        copy.start()
    one_state[spot] = state_ref[:, rows_of(spot), :]
    one_log[spot] = log_ref[...]
    for o, q in enumerate(others):
        remote(one_state.at[q], one_state.at[q], base + 2 * o, base + 2 * q, device).wait_recv()
        remote(one_log.at[q], one_log.at[q], base + 2 * o + 1, base + 2 * q + 1, device).wait_recv()

    decays = [[decay_of(one_log[q, d]) for q in range(mates)] for d in range(2)]
    orders = [list(range(mates)), list(range(mates))[::-1]]
    for d in range(2):
        total = None
        logs = None
        for q in orders[d]:
            part = one_state[q, d].astype(F32)
            log = one_log[q, d].astype(F32)
            total = part if total is None else total * decays[d][q] + part
            logs = log if logs is None else logs + log
        sum_state[d] = total.astype(BF16)
        sum_log[d] = packed_row(logs[0:1, :] + logs[1:2, :])
    base = 2 * mates
    for o, p in enumerate(far):
        d = jnp.where(p > plane, 0, 1)
        to = p * mates + spot
        for j, (source, target) in enumerate(((sum_state, two_state), (sum_log, two_log))):
            copy = remote(
                source.at[d], target.at[plane], base + 2 * o + j, base + 2 * plane + j, to
            )
            copy.start()
            started.append(copy)
    for o, p in enumerate(far):
        for j, target in enumerate((two_state, two_log)):
            remote(
                target.at[p], target.at[p], base + 2 * o + j, base + 2 * p + j, device
            ).wait_recv()
    entry[...] = jnp.zeros_like(entry)

    def link(d, p):
        entry[d] = entry[d] * decay_of(two_log[p]) + two_state[p].astype(F32)

    for p in range(planes):
        pl.when(p < plane)(functools.partial(link, 0, p))
        pl.when(planes - 1 - p > plane)(functools.partial(link, 1, planes - 1 - p))

    base = 2 * mates + 2 * planes
    for d in range(2):
        carried = entry[d]
        for q in orders[d]:
            mine[q, d] = carried.astype(BF16)
            if q != orders[d][-1]:
                carried = carried * decays[d][q] + one_state[q, d].astype(F32)
    for o, q in enumerate(others):
        copy = remote(mine.at[q], three_state.at[spot], base + o, base + spot, plane * mates + q)
        copy.start()
        started.append(copy)
    three_state[spot] = mine[spot]
    for o, q in enumerate(others):
        remote(three_state.at[q], three_state.at[q], base + o, base + q, device).wait_recv()
    for q in range(mates):
        for d in range(2):
            out_ref[d, q * rows : (q + 1) * rows, :] = three_state[q, d].astype(F32)
    for copy in started:
        copy.wait_send()


def scan_kernel(
    width, d_ref, x_ref, gate_ref, b_ref, c_ref, raw_ref, params_ref, gain_ref, w_ref, carry_ref,
    part_ref, square_ref, state_ref, raw_scr, state_scr, summed,
):
    heads = raw_ref.shape[1]
    rows, channels = x_ref.shape[1:]
    d = d_ref[0]
    backward = d == 1
    params = params_ref[...]
    head_rows = raw_scr.shape[0]
    matrix = spreader(head_rows, channels, width)

    @pl.when(pl.program_id(0) == 0)
    def _():
        state_scr[...] = carry_ref[0]

    raw_scr[...] = jnp.zeros_like(raw_scr)
    raw_scr[:heads, :] = raw_ref[0].astype(F32)
    skip = spread(jnp.broadcast_to(params[:, 2:3], (head_rows, SUB)), matrix)[0:1, :]
    t_index = lax.broadcasted_iota(jnp.int32, (SUB, SUB), 0)
    s_index = lax.broadcasted_iota(jnp.int32, (SUB, SUB), 1)
    sign = 1 - 2 * d
    seen = (t_index - s_index) * sign >= 0
    lane = lax.broadcasted_iota(jnp.int32, (SUB, 2 * width), 1)
    low = jnp.where(lane < width, 1.0, 0.0).astype(BF16)
    high = jnp.where(lane >= width, 1.0, 0.0).astype(BF16)
    subs = rows // SUB
    for i in range(subs):
        at = pl.multiple_of((i + d * (subs - 1 - 2 * i)) * SUB, SUB)
        here = pl.ds(at, SUB)
        step, log_decay = steps_of(raw_scr[:, here], params)
        cumulative, total = cumulate(log_decay, backward)
        rowterm = cumulative - jnp.log(step)
        columns = cumulative.T
        entry_decay = spread(jnp.exp(cumulative), matrix)
        tail = spread(jnp.exp(total - cumulative) * step, matrix)
        read = c_ref[0, 0, here, :]
        write = b_ref[0, 0, here, :]
        scores = lax.dot_general(
            read, write, (((1,), (1,)), ((), ())), preferred_element_type=F32
        )
        x = x_ref[0, here, :]
        wide = x.astype(F32)
        carried = jnp.dot(read, state_scr[...].astype(BF16), preferred_element_type=F32)
        summed[here, :] = carried * entry_decay + skip * wide
        for first in range(0, heads, 2):
            weights = []
            for h in range(first, min(first + 2, heads)):
                power = jnp.where(seen, columns[:, h : h + 1] - rowterm[h : h + 1, :], -1e30)
                weights.append((jnp.exp(power) * scores).astype(BF16))
            span = slice(first * width, (first + len(weights)) * width)
            some_x = x[:, span]
            if len(weights) == 2:
                weights = [jnp.concatenate(weights, axis=1)]
                some_x = jnp.concatenate([some_x * low, some_x * high], axis=0)
            summed[here, span] += jnp.dot(weights[0], some_x, preferred_element_type=F32)
        fresh = lax.dot_general(
            write, (wide * tail).astype(BF16), (((0,), (0,)), ((), ())),
            preferred_element_type=F32,
        )
        decay = jnp.where(backward, entry_decay[0:1, :], entry_decay[SUB - 1 :, :])
        state_scr[...] = state_scr[...] * decay + fresh

    @pl.when(pl.program_id(0) == pl.num_programs(0) - 1)
    def _():
        state_ref[0] = state_scr[...]

    scanned = summed[...].astype(BF16).astype(F32)
    gate = gate_ref[0].astype(F32)
    gated = scanned * (gate / (1.0 + jnp.exp(-gate)))
    squares = jnp.sum(gated * gated, axis=1, keepdims=True)
    square_ref[0] = jnp.broadcast_to(squares, (rows, SUB)).T[:8, :]
    part = jnp.dot(
        (gated * gain_ref[...]).astype(BF16), w_ref[...], preferred_element_type=F32
    ).astype(BF16)

    @pl.when(d == 0)
    def _():
        part_ref[...] = part

    @pl.when(d == 1)
    def _():
        flip = jnp.where(t_index + s_index == SUB - 1, 1.0, 0.0).astype(BF16)
        blocks = part.shape[1] // SUB
        for k in range(blocks):
            taken = part[:, (blocks - 1 - k) * SUB : (blocks - k) * SUB]
            part_ref[:, k * SUB : (k + 1) * SUB] = jnp.dot(
                taken, flip, preferred_element_type=F32
            ).astype(BF16)


def finish_kernel(inner, d_ref, own_ref, square_ref, part_ref, other_ref, out_ref):
    rows = own_ref.shape[0]
    total = square_ref[0] + other_ref[0]
    scale = lax.rsqrt(total / inner + EPS)
    scale = jnp.broadcast_to(scale[0:1, :], (SUB, rows)).T
    for k in range(own_ref.shape[1] // SUB):
        span = slice(k * SUB, (k + 1) * SUB)
        summed = own_ref[:, span].astype(F32) + part_ref[:, span].astype(F32)
        out_ref[:, span] = (summed * scale).astype(BF16)


def per_device(
    channels_in, gate_in, projections, step_raw, decay_log, step_bias, skip_gain, norm_gain,
    out_weight,
):
    tokens, channels = channels_in.shape[1:]
    heads = step_raw.shape[1]
    width = channels // heads
    state = projections.shape[-1]
    half = out_weight.shape[1]
    groups = lax.axis_size("head")
    inner = groups * channels
    devices = lax.axis_size("seq")
    block = 2 * SUB if tokens % (2 * SUB) == 0 else SUB
    blocks = tokens // block
    head_rows = padded(heads)
    params = jnp.pad(
        jnp.stack([decay_log, step_bias, skip_gain], axis=1), ((0, head_rows - heads), (0, 0))
    )

    totals, logs = pl.pallas_call(
        functools.partial(totals_kernel, width),
        out_shape=(
            jax.ShapeDtypeStruct((2, state, channels), BF16),
            jax.ShapeDtypeStruct((2, PAD, SUB), BF16),
        ),
        grid=(2,),
        in_specs=[
            pl.BlockSpec((1, tokens, channels), lambda d: (d, 0, 0)),
            pl.BlockSpec((1, 1, tokens, state), lambda d: (d, 0, 0, 0)),
            pl.BlockSpec((1, heads, tokens), lambda d: (d, 0, 0)),
            pl.BlockSpec((head_rows, 3), lambda d: (0, 0)),
        ],
        out_specs=[
            pl.BlockSpec((1, state, channels), lambda d: (d, 0, 0)),
            pl.BlockSpec((1, PAD, SUB), lambda d: (d, 0, 0)),
        ],
        scratch_shapes=[pltpu.VMEM((head_rows, tokens), F32), pltpu.VMEM((tokens, channels), BF16)],
        name="totals",
    )(channels_in, projections, step_raw, params)

    mates = math.gcd(devices, 4)
    planes = devices // mates
    share = state // mates
    copies = 3 * mates + 2 * planes
    carries = pl.pallas_call(
        functools.partial(carry_kernel, width, mates, planes),
        out_shape=jax.ShapeDtypeStruct((2, state, channels), F32),
        in_specs=[pl.BlockSpec(memory_space=pltpu.VMEM)] * 2,
        out_specs=pl.BlockSpec(memory_space=pltpu.VMEM),
        scratch_shapes=[
            pltpu.VMEM((mates, 2, share, channels), BF16),
            pltpu.VMEM((mates, 2, PAD, SUB), BF16),
            pltpu.VMEM((2, share, channels), BF16),
            pltpu.VMEM((2, PAD, SUB), BF16),
            pltpu.VMEM((planes, share, channels), BF16),
            pltpu.VMEM((planes, PAD, SUB), BF16),
            pltpu.VMEM((2, share, channels), F32),
            pltpu.VMEM((mates, 2, share, channels), BF16),
            pltpu.VMEM((mates, 2, share, channels), BF16),
            pltpu.SemaphoreType.DMA((copies,)),
            pltpu.SemaphoreType.DMA((copies,)),
        ],
        compiler_params=pltpu.CompilerParams(collective_id=0, has_side_effects=True),
        name="carry",
    )(totals, logs)

    def place(k, d):
        return k + d[0] * (blocks - 1 - 2 * k)

    def scan(d, first, count, entering, pick):
        whole = count == blocks

        def at(k, d):
            return place(first + k, d)

        def to(k, d):
            return place(k, d) if whole else k

        return pl.pallas_call(
            functools.partial(scan_kernel, width),
            out_shape=(
                jax.ShapeDtypeStruct((count * block, half), BF16),
                jax.ShapeDtypeStruct((count, 8, block), F32),
                jax.ShapeDtypeStruct((1, state, channels), F32),
            ),
            grid_spec=pltpu.PrefetchScalarGridSpec(
                num_scalar_prefetch=1,
                grid=(count,),
                in_specs=[
                    pl.BlockSpec((1, block, channels), lambda k, d: (d[0], at(k, d), 0)),
                    pl.BlockSpec((1, block, channels), lambda k, d: (d[0], at(k, d), 0)),
                    pl.BlockSpec((1, 1, block, state), lambda k, d: (d[0], 0, at(k, d), 0)),
                    pl.BlockSpec((1, 1, block, state), lambda k, d: (d[0], 1, at(k, d), 0)),
                    pl.BlockSpec((1, heads, block), lambda k, d: (d[0], 0, at(k, d))),
                    pl.BlockSpec((head_rows, 3), lambda k, d: (0, 0)),
                    pl.BlockSpec((1, channels), lambda k, d: (0, 0)),
                    pl.BlockSpec((channels, half), lambda k, d: (0, 0)),
                    pl.BlockSpec(
                        (1, state, channels), lambda k, d: (d[0] if pick else 0, 0, 0)
                    ),
                ],
                out_specs=[
                    pl.BlockSpec((block, half), lambda k, d: (to(k, d), 0)),
                    pl.BlockSpec((1, 8, block), lambda k, d: (to(k, d), 0, 0)),
                    pl.BlockSpec((1, state, channels), lambda k, d: (0, 0, 0)),
                ],
                scratch_shapes=[
                    pltpu.VMEM((head_rows, block), F32),
                    pltpu.VMEM((state, channels), F32),
                    pltpu.VMEM((block, channels), F32),
                ],
            ),
            cost_estimate=pl.CostEstimate(
                flops=8 * count * block * channels * half,
                bytes_accessed=6 * count * block * channels + 2 * channels * half,
                transcendentals=0,
            ),
            name="scan",
        )(
            d.astype(jnp.int32).reshape(1), channels_in, gate_in, projections, projections,
            step_raw, params, norm_gain[None], out_weight, entering,
        )

    def finish(d, k, own, squares, part, others):
        return pl.pallas_call(
            functools.partial(finish_kernel, inner),
            out_shape=jax.ShapeDtypeStruct(own.shape, BF16),
            grid_spec=pltpu.PrefetchScalarGridSpec(
                num_scalar_prefetch=1,
                grid=(1,),
                in_specs=[
                    pl.BlockSpec((block, half), lambda i, d: (place(k, d), 0)),
                    pl.BlockSpec((1, 8, block), lambda i, d: (place(k, d), 0, 0)),
                    pl.BlockSpec((block, half), lambda i, d: (0, 0)),
                    pl.BlockSpec((1, 8, block), lambda i, d: (0, 0, 0)),
                ],
                out_specs=pl.BlockSpec((block, half), lambda i, d: (place(k, d), 0)),
            ),
            input_output_aliases={1: 0},
            cost_estimate=pl.CostEstimate(
                flops=4 * block * half, bytes_accessed=6 * block * half, transcendentals=0
            ),
            name="finish",
        )(d.astype(jnp.int32).reshape(1), own, squares, part, others)

    group = lax.axis_index("head")
    if groups == 2:
        swap = [(0, 1), (1, 0)]
        arrived = []
        entering, pick = carries, True
        for k in range(blocks):
            part, squares, entering = scan(1 - group, k, 1, entering, pick)
            pick = False
            arrived.append((lax.ppermute(part, "head", swap), lax.ppermute(squares, "head", swap)))
        own, squares, _ = scan(group, 0, blocks, carries, True)
        for k, (part, others) in enumerate(arrived):
            own = finish(group, k, own, squares, part, others)
        return own
    results = [scan(jnp.asarray(d), 0, blocks, carries, True) for d in range(2)]
    summed = lax.psum_scatter(
        jnp.concatenate([results[0][0], results[1][0]], axis=1),
        "head", scatter_dimension=1, tiled=True,
    ).astype(F32)
    both = lax.psum(jnp.stack([results[0][1][:, 0], results[1][1][:, 0]]), "head")
    squares = jnp.where(2 * group >= groups, both[1], both[0]).reshape(tokens, 1)
    return (summed * lax.rsqrt(squares / inner + EPS)).astype(BF16)


def solution(mesh):
    placed = (
        P(None, "seq", "head"),
        P(None, "seq", "head"),
        P(None, None, "seq", None),
        P(None, "head", "seq"),
        P("head"),
        P("head"),
        P("head"),
        P("head"),
        P("head", None),
    )
    return jax.shard_map(
        per_device, mesh=mesh, in_specs=placed, out_specs=P("seq", "head"), check_vma=False
    )
```

```python
import functools
import math

import jax
import jax.numpy as jnp
from jax import lax
from jax.experimental import pallas as pl
from jax.experimental.pallas import tpu as pltpu
from jax.sharding import PartitionSpec as P

SUB = 128
PAD = 16
EPS = 1e-05
F32 = jnp.float32
BF16 = jnp.bfloat16


def padded(heads):
    return -(-heads // 8) * 8


def cumulate(values, backward):
    lane = lax.broadcasted_iota(jnp.int32, values.shape, 1)
    own = values
    reach = 1
    while reach < SUB:
        values = values + jnp.where(lane >= reach, pltpu.roll(values, reach, axis=1), 0.0)
        reach *= 2
    total = jnp.broadcast_to(values[:, SUB - 1 :], values.shape)
    if isinstance(backward, bool):
        return (total - values + own if backward else values), total
    return jnp.where(backward, total - values + own, values), total


def steps_of(raw, params):
    step = raw + params[:, 1:2]
    step = jnp.maximum(step, 0.0) + jnp.log1p(jnp.exp(-jnp.abs(step)))
    return step, -step * jnp.exp(params[:, 0:1])


def spreader(rows, columns, width):
    row = lax.broadcasted_iota(jnp.int32, (rows, columns), 0) * width
    column = lax.broadcasted_iota(jnp.int32, (rows, columns), 1)
    one = jnp.where((column >= row) & (column < row + width), 1.0, 0.0)
    return jnp.concatenate([one, one], axis=0).astype(BF16)


def spread(by_head, spread_matrix):
    high = by_head.astype(BF16).astype(F32)
    both = jnp.concatenate([high, by_head - high], axis=0).T.astype(BF16)
    return jnp.dot(both, spread_matrix, preferred_element_type=F32)


def totals_kernel(
    width, x_ref, b_ref, raw_ref, params_ref, out_ref, log_ref, raw_scr, scaled
):
    heads = raw_ref.shape[1]
    tokens, channels = x_ref.shape[1:]
    state = b_ref.shape[-1]
    raw_scr[...] = jnp.zeros_like(raw_scr)
    raw_scr[:heads, :] = raw_ref[0].astype(F32)
    params = params_ref[...]
    matrix = spreader(raw_scr.shape[0], channels, width)
    backward = pl.program_id(0) == 1
    count = tokens // SUB
    pieces = []
    everything = jnp.zeros((raw_scr.shape[0], SUB), F32)
    for k in range(count):
        step, log_decay = steps_of(raw_scr[:, k * SUB : (k + 1) * SUB], params)
        cumulative, total = cumulate(log_decay, backward)
        pieces.append((step, cumulative, total))
        everything = everything + total
    zero = jnp.zeros_like(everything)
    earlier, later = [zero], [zero]
    for k in range(count - 1):
        earlier.append(earlier[-1] + pieces[k][2])
        later.append(later[-1] + pieces[count - 1 - k][2])
    for k in range(count):
        step, cumulative, total = pieces[k]
        rest = jnp.where(backward, earlier[k], later[count - 1 - k])
        tail = jnp.exp(rest + total - cumulative) * step
        rows = slice(k * SUB, (k + 1) * SUB)
        scaled[rows, :] = (x_ref[0, rows, :].astype(F32) * spread(tail, matrix)).astype(BF16)
    summed = lax.dot_general(
        b_ref[0, 0], scaled[...], (((0,), (0,)), ((), ())), preferred_element_type=F32
    )
    out_ref[0] = summed.astype(BF16)
    rest = jnp.zeros((SUB - everything.shape[0], SUB), F32)
    log_ref[0] = packed_row(jnp.concatenate([everything, rest], axis=0).T[0:1, :])


def packed_row(row):
    row = jnp.broadcast_to(row, (PAD, row.shape[1]))
    high = row.astype(BF16).astype(F32)
    index = lax.broadcasted_iota(jnp.int32, row.shape, 0)
    return jnp.where(index == 0, high, jnp.where(index == 1, row - high, 0.0)).astype(BF16)


def carry_kernel(
    width, mates, planes, turns, state_ref, log_ref, out_ref, one_state, one_log, sum_state, sum_log,
    two_state, two_log, entry, mine, three_state, send_sem, recv_sem,
):
    device = lax.axis_index("seq")
    plane, spot = device // mates, device % mates
    rows = one_state.shape[3]
    span = 3 * mates + 2 * planes
    channels = state_ref.shape[-1]
    matrix = spreader(SUB, channels, width)[:SUB]

    def remote(source, target, which, slot, device_id):
        return pltpu.make_async_remote_copy(
            src_ref=source, dst_ref=target, send_sem=send_sem.at[which],
            recv_sem=recv_sem.at[slot], device_id={"seq": device_id},
            device_id_type=pl.DeviceIdType.MESH,
        )

    def rows_of(q, turn):
        return pl.ds(pl.multiple_of((q * turns + turn) * rows, rows), rows)

    def decay_of(packed):
        both = jnp.dot(packed, matrix, preferred_element_type=F32)
        return jnp.exp(both[0:1, :] + both[1:2, :])

    others = [(spot + o) % mates for o in range(1, mates)]
    far = [(plane + o) % planes for o in range(1, planes)]
    barrier = pltpu.get_barrier_semaphore()
    for q in others:
        pl.semaphore_signal(
            barrier, inc=1, device_id={"seq": plane * mates + q},
            device_id_type=pl.DeviceIdType.MESH,
        )
    for p in far:
        pl.semaphore_signal(
            barrier, inc=1, device_id={"seq": p * mates + spot},
            device_id_type=pl.DeviceIdType.MESH,
        )
    pl.semaphore_wait(barrier, mates + planes - 2)

    orders = [list(range(mates)), list(range(mates))[::-1]]
    started = []

    def begin(copy):
        copy.start()
        started.append(copy)

    for turn in range(turns):
        base = turn * span
        for o, q in enumerate(others):
            to = plane * mates + q
            begin(
                remote(
                    state_ref.at[:, rows_of(q, turn)], one_state.at[turn, spot], base + 2 * o,
                    base + 2 * spot, to,
                )
            )
            if turn == 0:
                begin(remote(log_ref, one_log.at[spot], 2 * o + 1, 2 * spot + 1, to))
        one_state[turn, spot] = state_ref[:, rows_of(spot, turn), :]
    one_log[spot] = log_ref[...]

    for turn in range(turns):
        base = turn * span
        for o, q in enumerate(others):
            target = one_state.at[turn, q]
            remote(target, target, base + 2 * o, base + 2 * q, device).wait_recv()
            if turn == 0:
                remote(one_log.at[q], one_log.at[q], 2 * o + 1, 2 * q + 1, device).wait_recv()
        if turn == 0:
            decays = [[decay_of(one_log[q, d]) for q in range(mates)] for d in range(2)]
        for d in range(2):
            total = None
            logs = None
            for q in orders[d]:
                part = one_state[turn, q, d].astype(F32)
                log = one_log[q, d].astype(F32)
                total = part if total is None else total * decays[d][q] + part
                logs = log if logs is None else logs + log
            sum_state[turn, d] = total.astype(BF16)
            if turn == 0:
                sum_log[d] = packed_row(logs[0:1, :] + logs[1:2, :])
        base = turn * span + 2 * mates
        for o, p in enumerate(far):
            d = jnp.where(p > plane, 0, 1)
            to = p * mates + spot
            begin(
                remote(
                    sum_state.at[turn, d], two_state.at[turn, plane], base + 2 * o,
                    base + 2 * plane, to,
                )
            )
            if turn == 0:
                begin(
                    remote(
                        sum_log.at[d], two_log.at[plane], base + 2 * o + 1, base + 2 * plane + 1, to
                    )
                )

    def link(turn, d, p):
        entry[turn, d] = entry[turn, d] * decay_of(two_log[p]) + two_state[turn, p].astype(F32)

    entry[...] = jnp.zeros_like(entry)
    for turn in range(turns):
        base = turn * span + 2 * mates
        for o, p in enumerate(far):
            target = two_state.at[turn, p]
            remote(target, target, base + 2 * o, base + 2 * p, device).wait_recv()
            if turn == 0:
                target = two_log.at[p]
                remote(target, target, base + 2 * o + 1, base + 2 * p + 1, device).wait_recv()
        for p in range(planes):
            last = planes - 1 - p
            pl.when(p < plane)(functools.partial(link, turn, 0, p))
            pl.when(last > plane)(functools.partial(link, turn, 1, last))
        base = turn * span + 2 * mates + 2 * planes
        for d in range(2):
            carried = entry[turn, d]
            for q in orders[d]:
                mine[turn, q, d] = carried.astype(BF16)
                if q != orders[d][-1]:
                    carried = carried * decays[d][q] + one_state[turn, q, d].astype(F32)
        for o, q in enumerate(others):
            begin(
                remote(
                    mine.at[turn, q], three_state.at[turn, spot], base + o, base + spot,
                    plane * mates + q,
                )
            )
        three_state[turn, spot] = mine[turn, spot]
    for turn in range(turns):
        base = turn * span + 2 * mates + 2 * planes
        for o, q in enumerate(others):
            target = three_state.at[turn, q]
            remote(target, target, base + o, base + q, device).wait_recv()
        for q in range(mates):
            at = (q * turns + turn) * rows
            for d in range(2):
                out_ref[d, at : at + rows, :] = three_state[turn, q, d].astype(F32)
    for copy in started:
        copy.wait_send()


def scan_kernel(
    width, d_ref, x_ref, gate_ref, b_ref, c_ref, raw_ref, params_ref, gain_ref, w_ref, carry_ref,
    part_ref, square_ref, state_ref, raw_scr, state_scr, summed,
):
    heads = raw_ref.shape[1]
    rows, channels = x_ref.shape[1:]
    d = d_ref[0]
    backward = d == 1
    params = params_ref[...]
    head_rows = raw_scr.shape[0]
    matrix = spreader(head_rows, channels, width)

    @pl.when(pl.program_id(0) == 0)
    def _():
        state_scr[...] = carry_ref[0]

    raw_scr[...] = jnp.zeros_like(raw_scr)
    raw_scr[:heads, :] = raw_ref[0].astype(F32)
    skip = spread(jnp.broadcast_to(params[:, 2:3], (head_rows, SUB)), matrix)[0:1, :]
    t_index = lax.broadcasted_iota(jnp.int32, (SUB, SUB), 0)
    s_index = lax.broadcasted_iota(jnp.int32, (SUB, SUB), 1)
    sign = 1 - 2 * d
    seen = (t_index - s_index) * sign >= 0
    lane = lax.broadcasted_iota(jnp.int32, (SUB, 2 * width), 1)
    low = jnp.where(lane < width, 1.0, 0.0).astype(BF16)
    high = jnp.where(lane >= width, 1.0, 0.0).astype(BF16)
    subs = rows // SUB
    for i in range(subs):
        at = pl.multiple_of((i + d * (subs - 1 - 2 * i)) * SUB, SUB)
        here = pl.ds(at, SUB)
        step, log_decay = steps_of(raw_scr[:, here], params)
        cumulative, total = cumulate(log_decay, backward)
        rowterm = cumulative - jnp.log(step)
        columns = cumulative.T
        entry_decay = spread(jnp.exp(cumulative), matrix)
        tail = spread(jnp.exp(total - cumulative) * step, matrix)
        read = c_ref[0, 0, here, :]
        write = b_ref[0, 0, here, :]
        scores = lax.dot_general(
            read, write, (((1,), (1,)), ((), ())), preferred_element_type=F32
        )
        x = x_ref[0, here, :]
        wide = x.astype(F32)
        carried = jnp.dot(read, state_scr[...].astype(BF16), preferred_element_type=F32)
        summed[here, :] = carried * entry_decay + skip * wide
        for first in range(0, heads, 2):
            weights = []
            for h in range(first, min(first + 2, heads)):
                power = jnp.where(seen, columns[:, h : h + 1] - rowterm[h : h + 1, :], -1e30)
                weights.append((jnp.exp(power) * scores).astype(BF16))
            span = slice(first * width, (first + len(weights)) * width)
            some_x = x[:, span]
            if len(weights) == 2:
                weights = [jnp.concatenate(weights, axis=1)]
                some_x = jnp.concatenate([some_x * low, some_x * high], axis=0)
            summed[here, span] += jnp.dot(weights[0], some_x, preferred_element_type=F32)
        fresh = lax.dot_general(
            write, (wide * tail).astype(BF16), (((0,), (0,)), ((), ())),
            preferred_element_type=F32,
        )
        decay = jnp.where(backward, entry_decay[0:1, :], entry_decay[SUB - 1 :, :])
        state_scr[...] = state_scr[...] * decay + fresh

    @pl.when(pl.program_id(0) == pl.num_programs(0) - 1)
    def _():
        state_ref[0] = state_scr[...]

    scanned = summed[...].astype(BF16).astype(F32)
    gate = gate_ref[0].astype(F32)
    gated = scanned * (gate / (1.0 + jnp.exp(-gate)))
    squares = jnp.sum(gated * gated, axis=1, keepdims=True)
    square_ref[0] = jnp.broadcast_to(squares, (rows, SUB)).T[:8, :]
    part = jnp.dot(
        (gated * gain_ref[...]).astype(BF16), w_ref[...], preferred_element_type=F32
    ).astype(BF16)

    @pl.when(d == 0)
    def _():
        part_ref[...] = part

    @pl.when(d == 1)
    def _():
        flip = jnp.where(t_index + s_index == SUB - 1, 1.0, 0.0).astype(BF16)
        blocks = part.shape[1] // SUB
        for k in range(blocks):
            taken = part[:, (blocks - 1 - k) * SUB : (blocks - k) * SUB]
            part_ref[:, k * SUB : (k + 1) * SUB] = jnp.dot(
                taken, flip, preferred_element_type=F32
            ).astype(BF16)


def finish_kernel(inner, count, d_ref, own_ref, square_ref, *refs):
    out_ref = refs[-1]
    rows = own_ref.shape[0]

    def finish(part_ref, other_ref):
        total = square_ref[0] + other_ref[0]
        scale = lax.rsqrt(total / inner + EPS)
        scale = jnp.broadcast_to(scale[0:1, :], (SUB, rows)).T
        for k in range(own_ref.shape[1] // SUB):
            span = slice(k * SUB, (k + 1) * SUB)
            summed = own_ref[:, span].astype(F32) + part_ref[:, span].astype(F32)
            out_ref[:, span] = (summed * scale).astype(BF16)

    for i in range(count):
        chosen = functools.partial(finish, refs[i], refs[count + i])
        pl.when(pl.program_id(0) == i)(chosen)


def per_device(
    channels_in, gate_in, projections, step_raw, decay_log, step_bias, skip_gain, norm_gain,
    out_weight,
):
    tokens, channels = channels_in.shape[1:]
    heads = step_raw.shape[1]
    width = channels // heads
    state = projections.shape[-1]
    half = out_weight.shape[1]
    groups = lax.axis_size("head")
    inner = groups * channels
    devices = lax.axis_size("seq")
    block = 2 * SUB if tokens % (2 * SUB) == 0 else SUB
    blocks = tokens // block
    head_rows = padded(heads)
    params = jnp.pad(
        jnp.stack([decay_log, step_bias, skip_gain], axis=1), ((0, head_rows - heads), (0, 0))
    )

    totals, logs = pl.pallas_call(
        functools.partial(totals_kernel, width),
        out_shape=(
            jax.ShapeDtypeStruct((2, state, channels), BF16),
            jax.ShapeDtypeStruct((2, PAD, SUB), BF16),
        ),
        grid=(2,),
        in_specs=[
            pl.BlockSpec((1, tokens, channels), lambda d: (d, 0, 0)),
            pl.BlockSpec((1, 1, tokens, state), lambda d: (d, 0, 0, 0)),
            pl.BlockSpec((1, heads, tokens), lambda d: (d, 0, 0)),
            pl.BlockSpec((head_rows, 3), lambda d: (0, 0)),
        ],
        out_specs=[
            pl.BlockSpec((1, state, channels), lambda d: (d, 0, 0)),
            pl.BlockSpec((1, PAD, SUB), lambda d: (d, 0, 0)),
        ],
        scratch_shapes=[pltpu.VMEM((head_rows, tokens), F32), pltpu.VMEM((tokens, channels), BF16)],
        name="totals",
    )(channels_in, projections, step_raw, params)

    mates = math.gcd(devices, 4)
    planes = devices // mates
    turns = 2
    share = state // mates // turns
    copies = turns * (3 * mates + 2 * planes)
    carries = pl.pallas_call(
        functools.partial(carry_kernel, width, mates, planes, turns),
        out_shape=jax.ShapeDtypeStruct((2, state, channels), F32),
        in_specs=[pl.BlockSpec(memory_space=pltpu.VMEM)] * 2,
        out_specs=pl.BlockSpec(memory_space=pltpu.VMEM),
        scratch_shapes=[
            pltpu.VMEM((turns, mates, 2, share, channels), BF16),
            pltpu.VMEM((mates, 2, PAD, SUB), BF16),
            pltpu.VMEM((turns, 2, share, channels), BF16),
            pltpu.VMEM((2, PAD, SUB), BF16),
            pltpu.VMEM((turns, planes, share, channels), BF16),
            pltpu.VMEM((planes, PAD, SUB), BF16),
            pltpu.VMEM((turns, 2, share, channels), F32),
            pltpu.VMEM((turns, mates, 2, share, channels), BF16),
            pltpu.VMEM((turns, mates, 2, share, channels), BF16),
            pltpu.SemaphoreType.DMA((copies,)),
            pltpu.SemaphoreType.DMA((copies,)),
        ],
        compiler_params=pltpu.CompilerParams(collective_id=0, has_side_effects=True),
        name="carry",
    )(totals, logs)

    def place(k, d):
        return k + d[0] * (blocks - 1 - 2 * k)

    def scan(d, first, count, entering, pick):
        whole = count == blocks

        def at(k, d):
            return place(first + k, d)

        def to(k, d):
            return place(k, d) if whole else k

        return pl.pallas_call(
            functools.partial(scan_kernel, width),
            out_shape=(
                jax.ShapeDtypeStruct((count * block, half), BF16),
                jax.ShapeDtypeStruct((count, 8, block), F32),
                jax.ShapeDtypeStruct((1, state, channels), F32),
            ),
            grid_spec=pltpu.PrefetchScalarGridSpec(
                num_scalar_prefetch=1,
                grid=(count,),
                in_specs=[
                    pl.BlockSpec((1, block, channels), lambda k, d: (d[0], at(k, d), 0)),
                    pl.BlockSpec((1, block, channels), lambda k, d: (d[0], at(k, d), 0)),
                    pl.BlockSpec((1, 1, block, state), lambda k, d: (d[0], 0, at(k, d), 0)),
                    pl.BlockSpec((1, 1, block, state), lambda k, d: (d[0], 1, at(k, d), 0)),
                    pl.BlockSpec((1, heads, block), lambda k, d: (d[0], 0, at(k, d))),
                    pl.BlockSpec((head_rows, 3), lambda k, d: (0, 0)),
                    pl.BlockSpec((1, channels), lambda k, d: (0, 0)),
                    pl.BlockSpec((channels, half), lambda k, d: (0, 0)),
                    pl.BlockSpec(
                        (1, state, channels), lambda k, d: (d[0] if pick else 0, 0, 0)
                    ),
                ],
                out_specs=[
                    pl.BlockSpec((block, half), lambda k, d: (to(k, d), 0)),
                    pl.BlockSpec((1, 8, block), lambda k, d: (to(k, d), 0, 0)),
                    pl.BlockSpec((1, state, channels), lambda k, d: (0, 0, 0)),
                ],
                scratch_shapes=[
                    pltpu.VMEM((head_rows, block), F32),
                    pltpu.VMEM((state, channels), F32),
                    pltpu.VMEM((block, channels), F32),
                ],
            ),
            cost_estimate=pl.CostEstimate(
                flops=8 * count * block * channels * half,
                bytes_accessed=6 * count * block * channels + 2 * channels * half,
                transcendentals=0,
            ),
            name="scan",
        )(
            d.astype(jnp.int32).reshape(1), channels_in, gate_in, projections, projections,
            step_raw, params, norm_gain[None], out_weight, entering,
        )

    def finish(d, first, arrived, own, squares):
        count = len(arrived)
        parts, others = zip(*arrived)
        return pl.pallas_call(
            functools.partial(finish_kernel, inner, count),
            out_shape=jax.ShapeDtypeStruct(own.shape, BF16),
            grid_spec=pltpu.PrefetchScalarGridSpec(
                num_scalar_prefetch=1,
                grid=(count,),
                in_specs=[
                    pl.BlockSpec((block, half), lambda i, d: (place(first + i, d), 0)),
                    pl.BlockSpec((1, 8, block), lambda i, d: (place(first + i, d), 0, 0)),
                    *[pl.BlockSpec((block, half), lambda i, d: (0, 0))] * count,
                    *[pl.BlockSpec((1, 8, block), lambda i, d: (0, 0, 0))] * count,
                ],
                out_specs=pl.BlockSpec((block, half), lambda i, d: (place(first + i, d), 0)),
            ),
            input_output_aliases={1: 0},
            cost_estimate=pl.CostEstimate(
                flops=4 * count * block * half, bytes_accessed=6 * count * block * half,
                transcendentals=0,
            ),
            name="finish",
        )(d.astype(jnp.int32).reshape(1), own, squares, *parts, *others)

    group = lax.axis_index("head")
    if groups == 2:
        swap = [(0, 1), (1, 0)]
        arrived = []
        entering, pick = carries, True
        for k in range(blocks):
            part, squares, entering = scan(1 - group, k, 1, entering, pick)
            pick = False
            arrived.append((lax.ppermute(part, "head", swap), lax.ppermute(squares, "head", swap)))
        own, squares, _ = scan(group, 0, blocks, carries, True)
        if blocks > 1:
            own = finish(group, 0, arrived[:-1], own, squares)
        return finish(group, blocks - 1, arrived[-1:], own, squares)
    results = [scan(jnp.asarray(d), 0, blocks, carries, True) for d in range(2)]
    summed = lax.psum_scatter(
        jnp.concatenate([results[0][0], results[1][0]], axis=1),
        "head", scatter_dimension=1, tiled=True,
    ).astype(F32)
    both = lax.psum(jnp.stack([results[0][1][:, 0], results[1][1][:, 0]]), "head")
    squares = jnp.where(2 * group >= groups, both[1], both[0]).reshape(tokens, 1)
    return (summed * lax.rsqrt(squares / inner + EPS)).astype(BF16)


def solution(mesh):
    placed = (
        P(None, "seq", "head"),
        P(None, "seq", "head"),
        P(None, None, "seq", None),
        P(None, "head", "seq"),
        P("head"),
        P("head"),
        P("head"),
        P("head"),
        P("head", None),
    )
    return jax.shard_map(
        per_device, mesh=mesh, in_specs=placed, out_specs=P("seq", "head"), check_vma=False
    )
```
